32 devices in a mesh: groups: 2 (over x), node: 16 (over z, y, core).
Axes of the slice: x: 2, y: 2, z: 4, core: 2. Of those that a mesh axis runs over, the one named last changes fastest.
Arguments:
- tokens: bfloat16 [1024, 3584], P(('groups', 'node')), parts along dimension 0, may hold values from -6 to 6
- routes: int32 [1024, 8], P(('groups', 'node')), parts along dimension 0, may hold values from 0 to 15, all different within a row; in each aligned block of 32 rows (0 to 31, 32 to 63, ...) at most 32 rows name the same one
- gates: float32 [1024, 8], P(('groups', 'node')), parts along dimension 0, may hold values from 0.1 to 0.5
- w_gate: bfloat16 [16, 3584, 1024], P('node'), may hold values from -0.09375 to 0.09375
- w_up: bfloat16 [16, 3584, 1024], P('node'), may hold values from -0.09375 to 0.09375
- w_down: bfloat16 [16, 1024, 3584], P('node'), may hold values from -0.1875 to 0.1875
Outputs:
- mixed: bfloat16 [1024, 3584], P(('groups', 'node')), parts along dimension 0
The draws below stay inside these ranges and needn't reach their ends.
There are 2 independent parts, one for each index of `groups`. The reference program is written for one: setup_inputs(seed, part) draws one part's arguments, and reference() takes and returns one part's arrays. A program takes and returns all parts, laid end to end along the dimension named above; an argument that names none is the same for every part. Nothing has to cross between parts.
Inputs may be any that keep to these rules, and one draw needn't show every extreme that they name: `routes`: each token names 8 different experts; at most 32 of the tokens of one device name the same expert, and exactly 32 do so for some expert and device.
All inputs are finite; a program needn't handle non-finite values.
Results may differ from the reference program's by a relative error of at most 0.0057.
Values may be sent and summed in bfloat16 or wider, within the bound.
A program may use at most 128 MiB of HBM per device.

```python
import math
import jax
import jax.numpy as jnp
import numpy as np
from jax import lax

D = 3584
FF = 1024
TOPK = 8
TOK_DEV = 32
EXPERTS = 16
TOKENS = 512
MOST = 32
N_NODE = 16


def block_scale(stream_key, shape, cuts, low, high):
    factor_of, own = 1.0, jax.random.fold_in(stream_key, 6)
    for axis_at, parts in cuts:
        draws = jnp.exp(jax.random.uniform(jax.random.fold_in(own, axis_at), (parts,), jnp.float32, low / len(cuts), high / len(cuts)))
        factor_of = factor_of * jnp.repeat(draws, shape[axis_at] // parts).reshape([-1 if axis == axis_at else 1 for axis in range(len(shape))])
    return factor_of


def shared_out(own_key, own, number, rows, number_of, top, bound, slope):
    sequence = jax.random.permutation(own_key, number_of)
    heavy_load, ordinary = shares(number_of, rows * top, bound, slope, True), shares(number_of, rows * top, bound, slope, False)
    places = jnp.arange(number_of)

    def named(sizes, rotation):
        used = int((sizes > 0).sum())
        fixed = max(1, used // 4)
        passed = fixed + (places - fixed + rotation * (used - fixed)) % max(1, number_of - fixed)
        return jnp.zeros((number_of,), jnp.int32).at[sequence[jnp.where(places < fixed, places, passed)]].set(jnp.asarray(sizes, jnp.int32))

    sizes = jnp.where(number % 4 == 0, named(heavy_load, number // 4), named(ordinary, number - number // 4 - 1))
    mixed = jax.random.permutation(jax.random.fold_in(own, 3), number_of)
    source_of, receiver = mixed[0:number_of // 2 * 2:2], mixed[1:number_of // 2 * 2:2]
    slack = jnp.minimum(sizes[source_of] - 1, bound - sizes[receiver]) // 2
    slack = jnp.where((source_of == sequence[0]) | (receiver == sequence[0]) | (sizes[receiver] == 0), 0, jnp.maximum(slack, 0))
    passed = jax.random.randint(jax.random.fold_in(own, 4), (number_of // 2,), 0, 1 << 20) % (slack + 1)
    sizes = sizes.at[source_of].add(-passed).at[receiver].add(passed)
    labels = jnp.searchsorted(jnp.cumsum(sizes), jnp.arange(rows * top), side="right").astype(jnp.int32)
    listing = labels.reshape(top, rows).T
    listing = listing[jax.random.permutation(jax.random.fold_in(own, 1), rows)]
    rotation = jax.random.randint(jax.random.fold_in(own, 2), (rows, 1), 0, top)
    return jnp.take_along_axis(listing, (jnp.arange(top)[None, :] + rotation) % top, axis=1)


def shares(count, total, most, slope, full):
    weights = [(1 << 20) // math.isqrt(standing ** slope) + 1 for standing in range(1, count + 1)]
    largest = most if full else min(most, max(-(-total // count), total * weights[0] // sum(weights)))
    least = 1 if total - largest >= count - 1 else 0
    given, rest = [largest] + [least] * (count - 1), total - largest - least * (count - 1)
    while rest > 0:
        movable = [i for i in range(1, count) if given[i] < largest] or [i for i in range(1, count) if given[i] < most]
        pool, budget = sum([weights[i] for i in movable]), rest
        for i in movable:
            extra = min(most - given[i], max(1, budget * weights[i] // pool), rest)
            given[i] = given[i] + extra
            rest = rest - extra
    return np.array(given)


def scatter_about(key, dims, spread, limit, cuts=(), held_as=jnp.bfloat16):
    level = block_scale(key, dims, cuts, -0.22, 0.18) if cuts else 1.0
    drawn = jax.random.normal(key, dims, jnp.float32) * spread * level
    return jnp.minimum(jnp.maximum(drawn, -limit), limit).astype(held_as)


def setup_inputs(seed: int = 0, part: int = 0) -> dict:
    seeds = jax.random.split(jax.random.key(seed), 7)
    part_splits = jax.random.split(jax.random.fold_in(seeds[6], part), 7)
    tokens = scatter_about(part_splits[0], (TOKENS, D), 1.0, 6.0, ((0, 16),))
    routes_keys = jax.random.split(jax.random.fold_in(part_splits[1], 1), TOKENS // TOK_DEV)
    routes_turns = jax.random.permutation(jax.random.fold_in(part_splits[1], 3), TOKENS // TOK_DEV)
    routes = jax.vmap(lambda own, number: shared_out(jax.random.fold_in(part_splits[1], 2), own, number, TOK_DEV, EXPERTS, TOPK, MOST, 2))(routes_keys, routes_turns).reshape((TOKENS, TOPK))
    gates = jnp.clip(0.1 + 0.4 * jax.random.uniform(part_splits[2], (TOKENS, TOPK), jnp.float32) ** block_scale(part_splits[2], (TOKENS, TOPK), ((0, 16),), -0.2, 0.2), 0.1, 0.5)
    w_gate = scatter_about(seeds[3], (EXPERTS, D, FF), D ** -0.5, 0.09375, ((0, 16),))
    w_up = scatter_about(seeds[4], (EXPERTS, D, FF), D ** -0.5, 0.09375, ((0, 16),))
    w_down = scatter_about(seeds[5], (EXPERTS, FF, D), FF ** -0.5, 0.1875, ((0, 16),))
    return {"tokens": tokens, "routes": routes, "gates": gates, "w_gate": w_gate, "w_up": w_up, "w_down": w_down}


def reference(tokens, routes, gates, w_gate, w_up, w_down):
    capacity = N_NODE * MOST
    order = jnp.arange(TOKENS, dtype=jnp.int32)

    def one_expert(total, inputs):
        expert_id, gate_mat, up_mat, down_mat = inputs
        hits = routes == expert_id
        weight = jnp.sum(jnp.where(hits, gates, jnp.zeros_like(gates)), axis=1)
        routed = jnp.any(hits, axis=1)
        score = jnp.where(routed, 2 * TOKENS, 0).astype(jnp.int32) + (TOKENS - order)
        picked = lax.top_k(score, capacity)[1].astype(jnp.int32)
        rows = tokens[picked]
        gate = jnp.dot(rows, gate_mat, preferred_element_type=jnp.float32)
        upper = jnp.dot(rows, up_mat, preferred_element_type=jnp.float32)
        hidden = (jax.nn.silu(gate) * upper).astype(jnp.bfloat16)
        produced = jnp.dot(hidden, down_mat, preferred_element_type=jnp.float32).astype(jnp.bfloat16)
        contrib = weight[picked][:, None] * produced.astype(weight.dtype)
        return total.at[picked].add(contrib), None

    start = jnp.zeros((TOKENS, D), gates.dtype)
    total, _ = lax.scan(one_expert, start, (jnp.arange(EXPERTS, dtype=jnp.int32), w_gate, w_up, w_down))
    return total.astype(jnp.bfloat16)
```

```python
import functools

import jax
import jax.numpy as jnp
from jax import lax
from jax.experimental import pallas as pl
from jax.experimental.pallas import tpu as pltpu
from jax.sharding import PartitionSpec as P

MESH = pl.DeviceIdType.MESH
PACK = 8
A, B, T = 0, 1, 2


def ring_order(chips, rows):
    if rows == 2 and chips % 2 == 0:
        length = chips // 2
        return [z * 2 for z in range(length)] + [z * 2 + 1 for z in reversed(range(length))]
    return list(range(chips))


def lookup(index, table):
    found = jnp.int32(0)
    for at, value in enumerate(table):
        found = found + jnp.where(index == at, value, 0)
    return found


def column(row, rows):
    at = lax.broadcasted_iota(jnp.int32, (rows, rows), 0)
    to = lax.broadcasted_iota(jnp.int32, (rows, rows), 1)
    return jnp.sum(jnp.where(at == to, jnp.broadcast_to(row, (rows, rows)), jnp.zeros((), row.dtype)), axis=1, keepdims=True)


def kernel(order, tok_ref, routes_ref, gates_ref, wg_hbm, wu_hbm, wd_hbm, out_ref,
           wg, wu, wd, x, tab, hid, mine, to_sib, from_sib, in_r, in_l, out_r, out_l,
           w_sem, ag_send, ag_recv, sf_send, sf_recv, rs_send, rs_recv, ps_send, ps_recv):
    chips = len(order)
    half = chips // 2
    experts = 2 * chips
    rows, width = tok_ref.shape
    ff = wg.shape[1]
    cut = rows // 2
    me = lax.axis_index("node")
    chip, core = me // 2, me % 2
    after, before = [0] * chips, [0] * chips
    for at in range(chips):
        after[order[at]] = order[(at + 1) % chips]
        before[order[at]] = order[(at - 1) % chips]
    right = lookup(chip, after) * 2 + core
    left = lookup(chip, before) * 2 + core
    sib = chip * 2 + (1 - core)

    loads = [pltpu.make_async_copy(src, dst, w_sem.at[at])
             for at, (src, dst) in enumerate(((wg_hbm, wg), (wu_hbm, wu), (wd_hbm, wd)))]
    for load in loads:
        load.start()

    barrier = pltpu.get_barrier_semaphore()
    for peer in (right, left, sib):
        pl.semaphore_signal(barrier, inc=1, device_id={"node": peer}, device_id_type=MESH)

    lanes = PACK * experts
    lane = lax.broadcasted_iota(jnp.int32, (rows, lanes), 1)
    sub = lax.broadcasted_iota(jnp.int32, (rows, lanes), 0) % PACK
    spread = jnp.zeros((rows, lanes), jnp.float32)
    for k in range(routes_ref.shape[0]):
        route, gate = column(routes_ref[k:k + 1, :], rows), column(gates_ref[k:k + 1, :], rows)
        spread = spread + jnp.where(lane == sub * experts + route, gate, 0.0)
    for at in range(rows // PACK):
        tab[0, at:at + 1, :] = jnp.sum(spread[at * PACK:(at + 1) * PACK], axis=0, keepdims=True)
    x[0:rows, :] = tok_ref[...]

    pl.semaphore_wait(barrier, 3)

    def place(offset):
        if offset == 0:
            return 0
        return 2 * offset - 1 if offset > 0 else -2 * offset

    def slot(offset, other):
        return 2 * place(offset) + other

    def offset_of(way, d):
        return half if d == half else (-d if way == 0 else d)

    def remote(src, dst, send, recv, peer):
        return pltpu.make_async_remote_copy(src_ref=src, dst_ref=dst, send_sem=send, recv_sem=recv,
                                            device_id={"node": peer}, device_id_type=MESH)

    def part(block, piece):
        return x.at[pl.ds(block * rows + piece * cut, cut), :]

    def hop(way, d, piece):
        to = slot(offset_of(way, d), 0)
        at = slot(offset_of(way, d - 1) if d > 1 else 0, 0)
        if piece == T:
            src, dst = tab.at[at], tab.at[to]
        else:
            src = tok_ref.at[pl.ds(piece * cut, cut), :] if d == 1 else part(at, piece)
            dst = part(to, piece)
        return remote(src, dst, ag_send.at[way, d - 1, piece], ag_recv.at[way, d - 1, piece], (right, left)[way])

    def travels(way, d, piece):
        if d < half:
            return True
        return piece in ((A, T) if way == 0 else (B,))

    started = []

    def go(copy):
        copy.start()
        started.append(copy)

    def share(at, offset):
        src, dst = slot(offset, 0), slot(offset, 1)
        blocks = (tok_ref if offset == 0 else x.at[pl.ds(src * rows, rows), :], x.at[pl.ds(dst * rows, rows), :])
        return [remote(*blocks, sf_send.at[at, 0], sf_recv.at[at, 0], sib),
                remote(tab.at[src], tab.at[dst], sf_send.at[at, 1], sf_recv.at[at, 1], sib)]

    for piece in (A, B, T):
        for way in (0, 1):
            go(hop(way, 1, piece))
    shares = {0: share(0, 0)}
    for copy in shares[0]:
        go(copy)

    def arrive(d, piece):
        for way in (0, 1):
            if not travels(way, d, piece):
                continue
            hop(way, d, piece).wait_recv()
            if d < half and travels(way, d + 1, piece):
                go(hop(way, d + 1, piece))

    def pass_on(d):
        for offset in ((d, -d) if d < half else (half,)):
            shares[offset] = share(place(offset), offset)
            for copy in shares[offset]:
                go(copy)

    def weight_of(block):
        packed = tab[block]
        full = jnp.concatenate([jnp.broadcast_to(packed[at:at + 1, :], (PACK, lanes)) for at in range(rows // PACK)], axis=0)
        return jnp.sum(jnp.where(lane == sub * experts + me, full, 0.0), axis=1, keepdims=True)

    tile_up = 512
    tile_down = 896 if width % 896 == 0 else 256

    def go_up(first, count, j):
        span = count * rows
        values = x.at[pl.ds(first * rows, span), :]

        def body(i, carry):
            cols = pl.ds(pl.multiple_of(i * tile_up, tile_up), tile_up)
            gate = jnp.dot(values[...], wg[:, cols], preferred_element_type=jnp.float32)
            upper = jnp.dot(values[...], wu[:, cols], preferred_element_type=jnp.float32)
            hid[0:span, cols] = (gate / (1.0 + jnp.exp(-gate)) * upper).astype(jnp.bfloat16)
            return carry

        tiles = ff // tile_up
        lax.fori_loop(j * tiles // 2, (j + 1) * tiles // 2, body, 0)

    def go_down(first, count):
        span = count * rows
        weights = [weight_of(first + at) for at in range(count)]

        def body(j, carry):
            cols = pl.ds(pl.multiple_of(j * tile_down, tile_down), tile_down)
            made = jnp.dot(hid[0:span, :], wd[:, cols], preferred_element_type=jnp.float32)
            made = made.astype(jnp.bfloat16).astype(jnp.float32)
            for at in range(count):
                value = made[at * rows:(at + 1) * rows] * weights[at]
                if at % 2 == 0:
                    mine[(first + at) // 2, :, cols] = value
                else:
                    to_sib[(first + at) // 2, :, cols] = value.astype(jnp.bfloat16)
            return carry

        lax.fori_loop(0, width // tile_down, body, 0)

    def group(d):
        if d == 1:
            return 0, 6
        return 4 * d - 2, (2 if d == half else 4)

    def chips_of(d):
        return ((0, 1, -1) if d == 1 else (d, -d)) if d < half else (half,)

    def up(d):
        for offset in chips_of(d):
            for copy in shares[offset]:
                copy.wait_recv()
        if d == 1:
            loads[0].wait()
            loads[1].wait()
        go_up(*group(d), 0)

    def up_rest(d):
        go_up(*group(d), 1)

    pair_copies = {}

    def down(d):
        if d == 1:
            loads[2].wait()
        first, count = group(d)
        go_down(first, count)
        span = pl.ds(first // 2, count // 2)
        pair_copies[d] = remote(to_sib.at[span], from_sib.at[span], ps_send.at[d - 1], ps_recv.at[d - 1], sib)
        go(pair_copies[d])

    for d in range(1, half):
        arrive(d, A)
        if d > 1:
            up(d - 1)
        arrive(d, B)
        arrive(d, T)
        pass_on(d)
        if d > 1:
            up_rest(d - 1)
            down(d - 1)
    up(half - 1)
    for piece in (A, B, T):
        arrive(half, piece)
    pass_on(half)
    up_rest(half - 1)
    down(half - 1)

    def chain(way, d, piece):
        rows_of = pl.ds(piece * cut, cut)
        src = (out_r, out_l)[way].at[d - 1, rows_of, :]
        dst = (in_r, in_l)[way].at[d - 1, rows_of, :]
        return remote(src, dst, rs_send.at[way, d - 1, piece], rs_recv.at[way, d - 1, piece], (right, left)[way])

    def starts(way, piece):
        return half if piece == way else half - 1

    def add_on(way, d, piece):
        at = place(offset_of(1 - way, d))
        rows_of = slice(piece * cut, (piece + 1) * cut)
        total = mine[at, rows_of, :] + from_sib[at, rows_of, :].astype(jnp.float32)
        if d < starts(way, piece):
            chain(way, d + 1, piece).wait_recv()
            total = total + (in_r, in_l)[way][d, rows_of, :].astype(jnp.float32)
        (out_r, out_l)[way][d - 1, rows_of, :] = total.astype(jnp.bfloat16)
        go(chain(way, d, piece))

    pair_copies[half - 1].wait_recv()
    for way in (0, 1):
        add_on(way, half - 1, 1 - way)
    up(half)
    up_rest(half)
    down(half)
    pair_copies[half].wait_recv()
    for way in (0, 1):
        add_on(way, half, way)
    for d in range(half - 2, 0, -1):
        pair_copies[d].wait_recv()
        for way in (0, 1):
            add_on(way, d, 1 - way)
        for way in (0, 1):
            add_on(way, d + 1, way)
    for way in (0, 1):
        add_on(way, 1, way)
    for piece in (A, B):
        rows_of = slice(piece * cut, (piece + 1) * cut)
        total = mine[0, rows_of, :] + from_sib[0, rows_of, :].astype(jnp.float32)
        for way in (0, 1):
            chain(way, 1, piece).wait_recv()
            total = total + (in_r, in_l)[way][0, rows_of, :].astype(jnp.float32)
        out_ref[rows_of, :] = total.astype(jnp.bfloat16)
    for copy in started:
        copy.wait_send()


def local(order, tokens, routes, gates, w_gate, w_up, w_down):
    rows, width = tokens.shape
    ff = w_gate.shape[2]
    chips = len(order)
    half = chips // 2
    bf16, f32 = jnp.bfloat16, jnp.float32
    dma = pltpu.SemaphoreType.DMA
    vmem = pl.BlockSpec(memory_space=pltpu.VMEM)
    hbm = pl.BlockSpec(memory_space=pl.ANY)
    return pl.pallas_call(
        functools.partial(kernel, order),
        out_shape=jax.ShapeDtypeStruct((rows, width), bf16),
        in_specs=[vmem] * 3 + [hbm] * 3,
        out_specs=vmem,
        scratch_shapes=[
            pltpu.VMEM((width, ff), bf16),
            pltpu.VMEM((width, ff), bf16),
            pltpu.VMEM((ff, width), bf16),
            pltpu.VMEM((2 * chips * rows, width), bf16),
            pltpu.VMEM((2 * chips, rows // PACK, PACK * 2 * chips), f32),
            pltpu.VMEM((6 * rows, ff), bf16),
            pltpu.VMEM((chips, rows, width), f32),
            pltpu.VMEM((chips, rows, width), bf16),
            pltpu.VMEM((chips, rows, width), bf16),
            pltpu.VMEM((half, rows, width), bf16),
            pltpu.VMEM((half, rows, width), bf16),
            pltpu.VMEM((half, rows, width), bf16),
            pltpu.VMEM((half, rows, width), bf16),
            dma((3,)),
            dma((2, half, 3)),
            dma((2, half, 3)),
            dma((chips, 2)),
            dma((chips, 2)),
            dma((2, half, 2)),
            dma((2, half, 2)),
            dma((half,)),
            dma((half,)),
        ],
        compiler_params=pltpu.CompilerParams(
            collective_id=0, has_side_effects=True, vmem_limit_bytes=67043328
        ),
    )(tokens, routes.T, gates.T, w_gate[0], w_up[0], w_down[0])


def solution(mesh):
    order = ring_order(mesh.shape["node"] // 2, 4 // mesh.shape["groups"])
    in_specs = (
        P(("groups", "node"), None),
        P(("groups", "node"), None),
        P(("groups", "node"), None),
        P("node", None, None),
        P("node", None, None),
        P("node", None, None),
    )
    out_specs = P(("groups", "node"), None)
    return jax.shard_map(
        functools.partial(local, order), mesh=mesh, in_specs=in_specs, out_specs=out_specs, check_vma=False
    )
```

```python
import functools

import jax
import jax.numpy as jnp
from jax import lax
from jax.experimental import pallas as pl
from jax.experimental.pallas import tpu as pltpu
from jax.sharding import PartitionSpec as P

MESH = pl.DeviceIdType.MESH
PACK = 8
PIECE = 512


def ring_order(chips, rows):
    if rows == 2 and chips % 2 == 0:
        length = chips // 2
        return [z * 2 for z in range(length)] + [z * 2 + 1 for z in reversed(range(length))]
    return list(range(chips))


def lookup(index, table):
    found = jnp.int32(0)
    for at, value in enumerate(table):
        found = found + jnp.where(index == at, value, 0)
    return found


def column(row, rows):
    at = lax.broadcasted_iota(jnp.int32, (rows, rows), 0)
    to = lax.broadcasted_iota(jnp.int32, (rows, rows), 1)
    return jnp.sum(jnp.where(at == to, jnp.broadcast_to(row, (rows, rows)), jnp.zeros((), row.dtype)), axis=1, keepdims=True)


def kernel(order, tok_hbm, routes_hbm, gates_hbm, wg_hbm, wu_hbm, wd_hbm, out_ref,
           wg, wu, wd, routes_ref, gates_ref, x, tab, hid, mine, to_sib, from_sib, in_r, in_l, out_r, out_l,
           w_sem, t_sem, ag_send, ag_recv, sf_send, sf_recv, rs_send, rs_recv, ps_send, ps_recv, ready, turn):
    chips = len(order)
    half = chips // 2
    experts = 2 * chips
    rows, width = tok_hbm.shape
    ff = wg.shape[1]
    pieces = width // PIECE
    me = lax.axis_index("node")
    chip, core = me // 2, me % 2
    after, before = [0] * chips, [0] * chips
    for at in range(chips):
        after[order[at]] = order[(at + 1) % chips]
        before[order[at]] = order[(at - 1) % chips]
    right = lookup(chip, after) * 2 + core
    left = lookup(chip, before) * 2 + core
    sib = chip * 2 + (1 - core)

    barrier = pltpu.get_barrier_semaphore()
    for peer in (right, left):
        pl.semaphore_signal(barrier, inc=1, device_id={"node": peer}, device_id_type=MESH)

    @pl.when(core == 0)
    def _():
        pl.semaphore_signal(barrier, inc=1, device_id={"node": sib}, device_id_type=MESH)

    lanes = PACK * experts
    lane = lax.broadcasted_iota(jnp.int32, (rows, lanes), 1)
    sub = lax.broadcasted_iota(jnp.int32, (rows, lanes), 0) % PACK

    def place(offset):
        if offset == 0:
            return 0
        return 2 * offset - 1 if offset > 0 else -2 * offset

    def offset_of(way, d):
        return half if d == half else (-d if way == 0 else d)

    def remote(src, dst, send, recv, peer):
        return pltpu.make_async_remote_copy(src_ref=src, dst_ref=dst, send_sem=send, recv_sem=recv,
                                            device_id={"node": peer}, device_id_type=MESH)

    def program(own):
        other = 1 - own
        started = []

        def go(copy):
            copy.start()
            started.append(copy)

        local = [pltpu.make_async_copy(routes_hbm, routes_ref, t_sem.at[0]),
                 pltpu.make_async_copy(gates_hbm, gates_ref, t_sem.at[1]),
                 pltpu.make_async_copy(tok_hbm, x.at[own, pl.ds(0, rows), :], t_sem.at[2])]
        loads = [pltpu.make_async_copy(src, dst, w_sem.at[at])
                 for at, (src, dst) in enumerate(((wg_hbm, wg), (wu_hbm, wu), (wd_hbm, wd)))]

        def table():
            local[0].wait()
            local[1].wait()
            spread = jnp.zeros((rows, lanes), jnp.float32)
            for k in range(routes_ref.shape[0]):
                route, gate = column(routes_ref[k:k + 1, :], rows), column(gates_ref[k:k + 1, :], rows)
                spread = spread + jnp.where(lane == sub * experts + route, gate, 0.0)
            for at in range(rows // PACK):
                tab[own, 0, at:at + 1, :] = jnp.sum(spread[at * PACK:(at + 1) * PACK], axis=0, keepdims=True)

        def side(piece):
            return pl.ds(piece * PIECE, PIECE)

        def part(block, piece):
            return x.at[own, pl.ds(block * rows, rows), side(piece)]

        def hop(way, d, piece):
            to = place(offset_of(way, d))
            at = place(offset_of(way, d - 1)) if d > 1 else 0
            if piece == pieces:
                src, dst = tab.at[own, at], tab.at[own, to]
            else:
                src = tok_hbm.at[:, side(piece)] if d == 1 else part(at, piece)
                dst = part(to, piece)
            return remote(src, dst, ag_send.at[way, d - 1, piece], ag_recv.at[way, d - 1, piece], (right, left)[way])

        def travels(way, d, piece):
            if d < half:
                return True
            return way == (0 if piece == pieces else piece % 2)

        def arrive(d, piece):
            for way in (0, 1):
                if not travels(way, d, piece):
                    continue
                hop(way, d, piece).wait_recv()
                if d < half and travels(way, d + 1, piece):
                    go(hop(way, d + 1, piece))

        def group(d):
            if d == 2:
                return 0, 5
            return 2 * d - 1, (1 if d == half else 2)

        def share(wave, d):
            first, count = group(d)
            block = pl.ds(first * rows, count * rows)
            return [remote(x.at[wave, block, :], x.at[wave, block, :], sf_send.at[d - 2, 0], sf_recv.at[d - 2, 0], sib),
                    remote(tab.at[wave, pl.ds(first, count)], tab.at[wave, pl.ds(first, count)],
                           sf_send.at[d - 2, 1], sf_recv.at[d - 2, 1], sib)]

        def pass_on(d):
            for copy in share(own, d):
                go(copy)

        def shared(*distances):
            for d in distances:
                for copy in share(other, d):
                    copy.wait_recv()

        parts = (group(2), (5, chips - 5))

        def rows_in(half_of):
            first, count = parts[half_of]
            return pl.ds(first * rows, count * rows)

        def go_up(wave, half_of, tile, i):
            cols = pl.ds(i * tile, tile)
            values = x.at[wave, rows_in(half_of), :]
            gate = jnp.dot(values[...], wg[:, cols], preferred_element_type=jnp.float32)
            upper = jnp.dot(values[...], wu[:, cols], preferred_element_type=jnp.float32)
            hid[rows_in(half_of), cols] = (gate / (1.0 + jnp.exp(-gate)) * upper).astype(jnp.bfloat16)

        def weights(wave, half_of):
            found = []
            first, count = parts[half_of]
            for block in range(first, first + count):
                packed = tab[wave, block]
                full = jnp.concatenate([jnp.broadcast_to(packed[at:at + 1, :], (PACK, lanes)) for at in range(rows // PACK)], axis=0)
                found.append(jnp.sum(jnp.where(lane == sub * experts + me, full, 0.0), axis=1, keepdims=True))
            return jnp.concatenate(found, axis=0)

        def go_down(wave, half_of, gains, piece):
            made = jnp.dot(hid[rows_in(half_of), :], wd[:, side(piece)], preferred_element_type=jnp.float32)
            made = made.astype(jnp.bfloat16).astype(jnp.float32) * gains
            if wave == own:
                mine[rows_in(half_of), side(piece)] = made
            else:
                to_sib[rows_in(half_of), side(piece)] = made.astype(jnp.bfloat16)

        def pair(half_of, piece):
            return remote(to_sib.at[rows_in(half_of), side(piece)], from_sib.at[rows_in(half_of), side(piece)],
                          ps_send.at[half_of, piece], ps_recv.at[half_of, piece], sib)

        def chain(way, d, piece):
            src = (out_r, out_l)[way].at[d - 1, :, side(piece)]
            dst = (in_r, in_l)[way].at[d - 1, :, side(piece)]
            return remote(src, dst, rs_send.at[way, d - 1, piece], rs_recv.at[way, d - 1, piece], (right, left)[way])

        def both(at, piece):
            rows_of = pl.ds(at * rows, rows)
            return mine[rows_of, side(piece)] + from_sib[rows_of, side(piece)].astype(jnp.float32)

        def add_on(step, piece):
            for way in (piece % 2, 1 - piece % 2):
                first = half if piece % 2 == way else half - 1
                d = first + 1 - step
                if d < 1:
                    continue
                total = both(place(offset_of(1 - way, d)), piece)
                if step > 1:
                    chain(way, d + 1, piece).wait_recv()
                    total = total + (in_r, in_l)[way][d, :, side(piece)].astype(jnp.float32)
                (out_r, out_l)[way][d - 1, :, side(piece)] = total.astype(jnp.bfloat16)
                go(chain(way, d, piece))

        def finish(piece):
            total = both(0, piece)
            for way in (0, 1):
                chain(way, 1, piece).wait_recv()
                total = total + (in_r, in_l)[way][0, :, side(piece)].astype(jnp.float32)
            out_ref[:, side(piece)] = total.astype(jnp.bfloat16)

        def interleaved(events, of):
            done = [0]

            def run(upto):
                upto = len(events) if upto is None else len(events) * upto // of
                for event in events[done[0]:upto]:
                    event()
                done[0] = max(done[0], upto)
            return run

        def multiply(wave, half_of, tile_up, run=None, upto=(0,) * 11):
            run = run or (lambda count: None)
            ups = ff // tile_up
            for i in range(ups):
                go_up(wave, half_of, tile_up, i)
                run(upto[(i + 1) * 4 // ups - 1])
            loaded(2)
            gains = weights(wave, half_of)
            for piece in range(pieces):
                go_down(wave, half_of, gains, piece)
                if wave == other:
                    go(pair(half_of, piece))
                elif half_of == 1 and piece > 0:
                    joined(piece - 1)
                run(upto[4 + piece * 7 // pieces])
            if wave == own and half_of == 1:
                joined(pieces - 1)

        def joined(piece):
            for half_of in (0, 1):
                pair(half_of, piece).wait_recv()
            add_on(1, piece)

        for copy in local:
            copy.start()
        for load in loads:
            load.start()

        def first_hops():
            for piece in range(pieces):
                for way in (0, 1):
                    go(hop(way, 1, piece))

        def first_table_hops():
            for way in (0, 1):
                go(hop(way, 1, pieces))

        waited = set()

        def loaded(*which):
            for at in which:
                if at not in waited:
                    loads[at].wait()
                    waited.add(at)

        def arrivals(d):
            found = [functools.partial(arrive, d, piece) for piece in range(pieces)]

            def rest():
                arrive(d, pieces)
                if d >= 2:
                    pass_on(d)
            return found + [rest]

        def steps(step):
            return [functools.partial(add_on, step, piece) for piece in range(pieces)]

        if own == 0:
            pl.semaphore_wait(barrier, 2)
            first_hops()
            table()
            first_table_hops()
            local[2].wait()
            for event in arrivals(1):
                event()
            events = arrivals(2)
            for event in events[:-1]:
                event()
            pl.semaphore_wait(ready, 1)
            pl.semaphore_signal(turn, inc=1, device_id={"node": sib}, device_id_type=MESH)
            events[-1]()
            run = interleaved([e for d in range(3, half + 1) for e in arrivals(d)], 16)
            loaded(0, 1)
            multiply(0, 0, 256, run, (1, 3, 5, 7, 8, 8, 9, 10, 11, 12, 13))
            run(None)
            multiply(0, 1, 512)
            run = interleaved([e for step in range(2, half + 1) for e in steps(step)], 21)
            shared(2)
            multiply(1, 0, 256, run, (0, 1, 3, 5, 6, 7, 7, 8, 9, 10, 11))
            shared(*range(3, half + 1))
            multiply(1, 1, 512, run, (11, 12, 13, 14, 14, 15, 15, 16, 16, 17, 17))
            run(None)
        else:
            pl.semaphore_wait(barrier, 3)
            pl.semaphore_signal(ready, inc=1, device_id={"node": sib}, device_id_type=MESH)
            table()
            local[2].wait()
            pl.semaphore_wait(turn, 1)
            first_hops()
            first_table_hops()
            run = interleaved([e for d in range(1, half + 1) for e in arrivals(d)], 32)
            loaded(0, 1)
            shared(2)
            multiply(0, 0, 256, run, (0, 2, 4, 7, 8, 8, 9, 9, 10, 10, 11))
            shared(*range(3, half + 1))
            multiply(0, 1, 256, run, (14, 16, 18, 20, 20, 21, 21, 22, 22, 23, 23))
            multiply(1, 0, 256, run, (24, 27, 30, 32, 32, 32, 32, 32, 32, 32, 32))
            run(None)
            multiply(1, 1, 512)
            for step in range(2, half + 1):
                for event in steps(step):
                    event()
        for piece in range(pieces):
            finish(piece)
        for copy in started:
            copy.wait_send()

    for own in (0, 1):
        pl.when(core == own)(functools.partial(program, own))


def local(order, tokens, routes, gates, w_gate, w_up, w_down):
    rows, width = tokens.shape
    ff = w_gate.shape[2]
    chips = len(order)
    half = chips // 2
    pieces = width // PIECE
    bf16, f32 = jnp.bfloat16, jnp.float32
    dma = pltpu.SemaphoreType.DMA
    vmem = pl.BlockSpec(memory_space=pltpu.VMEM)
    hbm = pl.BlockSpec(memory_space=pl.ANY)
    return pl.pallas_call(
        functools.partial(kernel, order),
        out_shape=jax.ShapeDtypeStruct((rows, width), bf16),
        in_specs=[hbm] * 6,
        out_specs=vmem,
        scratch_shapes=[
            pltpu.VMEM((width, ff), bf16),
            pltpu.VMEM((width, ff), bf16),
            pltpu.VMEM((ff, width), bf16),
            pltpu.VMEM(routes.shape[::-1], jnp.int32),
            pltpu.VMEM(gates.shape[::-1], f32),
            pltpu.VMEM((2, chips * rows, width), bf16),
            pltpu.VMEM((2, chips, rows // PACK, PACK * 2 * chips), f32),
            pltpu.VMEM((chips * rows, ff), bf16),
            pltpu.VMEM((chips * rows, width), f32),
            pltpu.VMEM((chips * rows, width), bf16),
            pltpu.VMEM((chips * rows, width), bf16),
            pltpu.VMEM((half, rows, width), bf16),
            pltpu.VMEM((half, rows, width), bf16),
            pltpu.VMEM((half, rows, width), bf16),
            pltpu.VMEM((half, rows, width), bf16),
            dma((3,)),
            dma((3,)),
            dma((2, half, pieces + 1)),
            dma((2, half, pieces + 1)),
            dma((half - 1, 2)),
            dma((half - 1, 2)),
            dma((2, half, pieces)),
            dma((2, half, pieces)),
            dma((2, pieces)),
            dma((2, pieces)),
            pltpu.SemaphoreType.REGULAR,
            pltpu.SemaphoreType.REGULAR,
        ],
        compiler_params=pltpu.CompilerParams(
            collective_id=0, has_side_effects=True, vmem_limit_bytes=67043328
        ),
    )(tokens, routes.T, gates.T, w_gate[0], w_up[0], w_down[0])


def solution(mesh):
    order = ring_order(mesh.shape["node"] // 2, 4 // mesh.shape["groups"])
    in_specs = (
        P(("groups", "node"), None),
        P(("groups", "node"), None),
        P(("groups", "node"), None),
        P("node", None, None),
        P("node", None, None),
        P("node", None, None),
    )
    out_specs = P(("groups", "node"), None)
    return jax.shard_map(
        functools.partial(local, order), mesh=mesh, in_specs=in_specs, out_specs=out_specs, check_vma=False
    )
```

```python
import functools

import jax
import jax.numpy as jnp
from jax import lax
from jax.experimental import pallas as pl
from jax.experimental.pallas import tpu as pltpu
from jax.sharding import PartitionSpec as P

MESH = pl.DeviceIdType.MESH
PACK = 8
PIECE = 512


def ring_order(chips, rows):
    if rows == 2 and chips % 2 == 0:
        length = chips // 2
        return [z * 2 for z in range(length)] + [z * 2 + 1 for z in reversed(range(length))]
    return list(range(chips))


def lookup(index, table):
    found = jnp.int32(0)
    for at, value in enumerate(table):
        found = found + jnp.where(index == at, value, 0)
    return found


def column(row, rows):
    at = lax.broadcasted_iota(jnp.int32, (rows, rows), 0)
    to = lax.broadcasted_iota(jnp.int32, (rows, rows), 1)
    return jnp.sum(jnp.where(at == to, jnp.broadcast_to(row, (rows, rows)), jnp.zeros((), row.dtype)), axis=1, keepdims=True)


def kernel(order, tok_hbm, routes_hbm, gates_hbm, wg_hbm, wu_hbm, wd_hbm, out_ref,
           wg, wu, wd, routes_ref, gates_ref, x, tab, hid, mine, to_sib, from_sib, in_r, in_l, out_r, out_l,
           w_sem, t_sem, ag_send, ag_recv, sf_send, sf_recv, rs_send, rs_recv, ps_send, ps_recv, ready, turn):
    chips = len(order)
    half = chips // 2
    experts = 2 * chips
    rows, width = tok_hbm.shape
    ff = wg.shape[1]
    pieces = width // PIECE
    me = lax.axis_index("node")
    chip, core = me // 2, me % 2
    after, before = [0] * chips, [0] * chips
    for at in range(chips):
        after[order[at]] = order[(at + 1) % chips]
        before[order[at]] = order[(at - 1) % chips]
    right = lookup(chip, after) * 2 + core
    left = lookup(chip, before) * 2 + core
    sib = chip * 2 + (1 - core)

    barrier = pltpu.get_barrier_semaphore()
    for peer in (right, left):
        pl.semaphore_signal(barrier, inc=1, device_id={"node": peer}, device_id_type=MESH)

    @pl.when(core == 0)
    def _():
        pl.semaphore_signal(barrier, inc=1, device_id={"node": sib}, device_id_type=MESH)

    lanes = PACK * experts
    lane = lax.broadcasted_iota(jnp.int32, (rows, lanes), 1)
    sub = lax.broadcasted_iota(jnp.int32, (rows, lanes), 0) % PACK

    def place(offset):
        if offset == 0:
            return 0
        return 2 * offset - 1 if offset > 0 else -2 * offset

    def offset_of(way, d):
        return half if d == half else (-d if way == 0 else d)

    def remote(src, dst, send, recv, peer):
        return pltpu.make_async_remote_copy(src_ref=src, dst_ref=dst, send_sem=send, recv_sem=recv,
                                            device_id={"node": peer}, device_id_type=MESH)

    def program(own):
        other = 1 - own
        started = []

        def go(copy):
            copy.start()
            started.append(copy)

        local = [pltpu.make_async_copy(routes_hbm, routes_ref, t_sem.at[0]),
                 pltpu.make_async_copy(gates_hbm, gates_ref, t_sem.at[1]),
                 pltpu.make_async_copy(tok_hbm, x.at[own, pl.ds(0, rows), :], t_sem.at[2])]
        loads = [pltpu.make_async_copy(src, dst, w_sem.at[at])
                 for at, (src, dst) in enumerate(((wg_hbm, wg), (wu_hbm, wu), (wd_hbm, wd)))]

        def table():
            local[0].wait()
            local[1].wait()
            spread = jnp.zeros((rows, lanes), jnp.float32)
            for k in range(routes_ref.shape[0]):
                route, gate = column(routes_ref[k:k + 1, :], rows), column(gates_ref[k:k + 1, :], rows)
                spread = spread + jnp.where(lane == sub * experts + route, gate, 0.0)
            for at in range(rows // PACK):
                tab[own, 0, at:at + 1, :] = jnp.sum(spread[at * PACK:(at + 1) * PACK], axis=0, keepdims=True)

        def side(piece):
            return pl.ds(piece * PIECE, PIECE)

        def part(block, piece):
            return x.at[own, pl.ds(block * rows, rows), side(piece)]

        def hop(way, d, piece):
            to = place(offset_of(way, d))
            at = place(offset_of(way, d - 1)) if d > 1 else 0
            if piece == pieces:
                src, dst = tab.at[own, at], tab.at[own, to]
            else:
                src = tok_hbm.at[:, side(piece)] if d == 1 else part(at, piece)
                dst = part(to, piece)
            return remote(src, dst, ag_send.at[way, d - 1, piece], ag_recv.at[way, d - 1, piece], (right, left)[way])

        def travels(way, d, piece):
            if d < half:
                return True
            return way == (0 if piece == pieces else piece % 2)

        def arrive(d, piece):
            for way in (0, 1):
                if not travels(way, d, piece):
                    continue
                hop(way, d, piece).wait_recv()
                if d < half and travels(way, d + 1, piece):
                    go(hop(way, d + 1, piece))

        def group(d):
            if d == 2:
                return 0, 5
            return 2 * d - 1, (1 if d == half else 2)

        def share(wave, d):
            first, count = group(d)
            block = pl.ds(first * rows, count * rows)
            return [remote(x.at[wave, block, :], x.at[wave, block, :], sf_send.at[d - 2, 0], sf_recv.at[d - 2, 0], sib),
                    remote(tab.at[wave, pl.ds(first, count)], tab.at[wave, pl.ds(first, count)],
                           sf_send.at[d - 2, 1], sf_recv.at[d - 2, 1], sib)]

        def pass_on(d):
            for copy in share(own, d):
                go(copy)

        def shared(*distances):
            for d in distances:
                for copy in share(other, d):
                    copy.wait_recv()

        parts = (group(2), (5, chips - 5))

        def rows_in(half_of):
            first, count = parts[half_of]
            return pl.ds(first * rows, count * rows)

        def go_up(wave, half_of, tile, i):
            cols = pl.ds(i * tile, tile)
            values = x.at[wave, rows_in(half_of), :]
            gate = jnp.dot(values[...], wg[:, cols], preferred_element_type=jnp.float32)
            upper = jnp.dot(values[...], wu[:, cols], preferred_element_type=jnp.float32)
            hid[rows_in(half_of), cols] = (gate / (1.0 + jnp.exp(-gate)) * upper).astype(jnp.bfloat16)

        def weights(wave, half_of):
            found = []
            first, count = parts[half_of]
            for block in range(first, first + count):
                packed = tab[wave, block]
                full = jnp.concatenate([jnp.broadcast_to(packed[at:at + 1, :], (PACK, lanes)) for at in range(rows // PACK)], axis=0)
                found.append(jnp.sum(jnp.where(lane == sub * experts + me, full, 0.0), axis=1, keepdims=True))
            return jnp.concatenate(found, axis=0)

        def go_down(wave, half_of, gains, piece):
            made = jnp.dot(hid[rows_in(half_of), :], wd[:, side(piece)], preferred_element_type=jnp.float32)
            made = made.astype(jnp.bfloat16).astype(jnp.float32) * gains
            if wave == own:
                mine[rows_in(half_of), side(piece)] = made
            else:
                to_sib[rows_in(half_of), side(piece)] = made.astype(jnp.bfloat16)

        def pair(half_of, piece):
            return remote(to_sib.at[rows_in(half_of), side(piece)], from_sib.at[rows_in(half_of), side(piece)],
                          ps_send.at[half_of, piece], ps_recv.at[half_of, piece], sib)

        def chain(way, d, piece):
            src = (out_r, out_l)[way].at[d - 1, :, side(piece)]
            dst = (in_r, in_l)[way].at[d - 1, :, side(piece)]
            return remote(src, dst, rs_send.at[way, d - 1, piece], rs_recv.at[way, d - 1, piece], (right, left)[way])

        def both(at, piece):
            rows_of = pl.ds(at * rows, rows)
            return mine[rows_of, side(piece)] + from_sib[rows_of, side(piece)].astype(jnp.float32)

        def add_on(step, piece):
            for way in (piece % 2, 1 - piece % 2):
                first = half if piece % 2 == way else half - 1
                d = first + 1 - step
                if d < 1:
                    continue
                total = both(place(offset_of(1 - way, d)), piece)
                if step > 1:
                    chain(way, d + 1, piece).wait_recv()
                    total = total + (in_r, in_l)[way][d, :, side(piece)].astype(jnp.float32)
                (out_r, out_l)[way][d - 1, :, side(piece)] = total.astype(jnp.bfloat16)
                go(chain(way, d, piece))

        def finish(piece):
            total = both(0, piece)
            for way in (0, 1):
                chain(way, 1, piece).wait_recv()
                total = total + (in_r, in_l)[way][0, :, side(piece)].astype(jnp.float32)
            out_ref[:, side(piece)] = total.astype(jnp.bfloat16)

        def interleaved(events, of):
            done = [0]

            def run(upto):
                upto = len(events) if upto is None else len(events) * upto // of
                for event in events[done[0]:upto]:
                    event()
                done[0] = max(done[0], upto)
            return run

        def multiply(wave, half_of, tile_up, run=None, upto=(0,) * 11):
            run = run or (lambda count: None)
            ups = ff // tile_up
            for i in range(ups):
                go_up(wave, half_of, tile_up, i)
                run(upto[(i + 1) * 4 // ups - 1])
            loaded(2)
            gains = weights(wave, half_of)
            for piece in range(pieces):
                go_down(wave, half_of, gains, piece)
                if wave == other:
                    go(pair(half_of, piece))
                elif half_of == 1 and piece > 0:
                    joined(piece - 1)
                run(upto[4 + piece * 7 // pieces])
            if wave == own and half_of == 1:
                joined(pieces - 1)

        def joined(piece):
            for half_of in (0, 1):
                pair(half_of, piece).wait_recv()
            add_on(1, piece)

        for copy in local:
            copy.start()
        for load in loads:
            load.start()

        def first_hops():
            for piece in range(pieces):
                for way in (0, 1):
                    go(hop(way, 1, piece))

        def first_table_hops():
            for way in (0, 1):
                go(hop(way, 1, pieces))

        waited = set()

        def loaded(*which):
            for at in which:
                if at not in waited:
                    loads[at].wait()
                    waited.add(at)

        def arrivals(d):
            found = [functools.partial(arrive, d, piece) for piece in range(pieces)]

            def rest():
                arrive(d, pieces)
                if d >= 2:
                    pass_on(d)
            return found + [rest]

        def steps(step):
            return [functools.partial(add_on, step, piece) for piece in range(pieces)]

        if own == 0:
            pl.semaphore_wait(barrier, 2)
            first_hops()
            table()
            first_table_hops()
            local[2].wait()
            for event in arrivals(1):
                event()
            events = arrivals(2)
            for event in events[:-1]:
                event()
            pl.semaphore_wait(ready, 1)
            pl.semaphore_signal(turn, inc=1, device_id={"node": sib}, device_id_type=MESH)
            events[-1]()
            run = interleaved([e for d in range(3, half + 1) for e in arrivals(d)], 16)
            loaded(0, 1)
            multiply(0, 0, 256, run, (1, 3, 5, 7, 8, 8, 9, 10, 11, 12, 13))
            run(None)
            multiply(0, 1, 512)
            run = interleaved([e for step in range(2, half + 1) for e in steps(step)], 21)
            shared(2)
            multiply(1, 0, 256, run, (0, 1, 3, 5, 6, 7, 7, 8, 9, 10, 11))
            shared(*range(3, half + 1))
            multiply(1, 1, 512, run, (11, 12, 13, 14, 14, 15, 15, 16, 16, 17, 17))
            run(None)
        else:
            pl.semaphore_wait(barrier, 3)
            pl.semaphore_signal(ready, inc=1, device_id={"node": sib}, device_id_type=MESH)
            table()
            local[2].wait()
            pl.semaphore_wait(turn, 1)
            first_hops()
            first_table_hops()
            run = interleaved([e for d in range(1, half + 1) for e in arrivals(d)], 32)
            loaded(0, 1)
            shared(2)
            multiply(0, 0, 256, run, (0, 2, 4, 7, 8, 8, 9, 9, 10, 10, 11))
            shared(*range(3, half + 1))
            multiply(0, 1, 256, run, (14, 16, 18, 20, 20, 21, 21, 22, 22, 23, 23))
            multiply(1, 0, 256, run, (24, 27, 30, 32, 32, 32, 32, 32, 32, 32, 32))
            run(None)
            multiply(1, 1, 512)
            for step in range(2, half + 1):
                for event in steps(step):
                    event()
        for piece in range(pieces):
            finish(piece)
        for copy in started:
            copy.wait_send()

    for own in (0, 1):
        pl.when(core == own)(functools.partial(program, own))


def local(order, tokens, routes, gates, w_gate, w_up, w_down):
    rows, width = tokens.shape
    ff = w_gate.shape[2]
    chips = len(order)
    half = chips // 2
    pieces = width // PIECE
    bf16, f32 = jnp.bfloat16, jnp.float32
    dma = pltpu.SemaphoreType.DMA
    vmem = pl.BlockSpec(memory_space=pltpu.VMEM)
    hbm = pl.BlockSpec(memory_space=pl.ANY)
    return pl.pallas_call(
        functools.partial(kernel, order),
        out_shape=pltpu.VMEM((rows, width), bf16),
        in_specs=[hbm] * 6,
        out_specs=vmem,
        scratch_shapes=[
            pltpu.VMEM((width, ff), bf16),
            pltpu.VMEM((width, ff), bf16),
            pltpu.VMEM((ff, width), bf16),
            pltpu.VMEM(routes.shape[::-1], jnp.int32),
            pltpu.VMEM(gates.shape[::-1], f32),
            pltpu.VMEM((2, chips * rows, width), bf16),
            pltpu.VMEM((2, chips, rows // PACK, PACK * 2 * chips), f32),
            pltpu.VMEM((chips * rows, ff), bf16),
            pltpu.VMEM((chips * rows, width), f32),
            pltpu.VMEM((chips * rows, width), bf16),
            pltpu.VMEM((chips * rows, width), bf16),
            pltpu.VMEM((half, rows, width), bf16),
            pltpu.VMEM((half, rows, width), bf16),
            pltpu.VMEM((half, rows, width), bf16),
            pltpu.VMEM((half, rows, width), bf16),
            dma((3,)),
            dma((3,)),
            dma((2, half, pieces + 1)),
            dma((2, half, pieces + 1)),
            dma((half - 1, 2)),
            dma((half - 1, 2)),
            dma((2, half, pieces)),
            dma((2, half, pieces)),
            dma((2, pieces)),
            dma((2, pieces)),
            pltpu.SemaphoreType.REGULAR,
            pltpu.SemaphoreType.REGULAR,
        ],
        compiler_params=pltpu.CompilerParams(
            collective_id=0, has_side_effects=True, vmem_limit_bytes=58720256
        ),
    )(tokens, routes.T, gates.T, w_gate[0], w_up[0], w_down[0])


def solution(mesh):
    order = ring_order(mesh.shape["node"] // 2, 4 // mesh.shape["groups"])
    in_specs = (
        P(("groups", "node"), None),
        P(("groups", "node"), None),
        P(("groups", "node"), None),
        P("node", None, None),
        P("node", None, None),
        P("node", None, None),
    )
    out_specs = P(("groups", "node"), None)
    return jax.shard_map(
        functools.partial(local, order), mesh=mesh, in_specs=in_specs, out_specs=out_specs, check_vma=False
    )
```

```python
import functools

import jax
import jax.numpy as jnp
from jax import lax
from jax.experimental import pallas as pl
from jax.experimental.pallas import tpu as pltpu
from jax.sharding import PartitionSpec as P

MESH = pl.DeviceIdType.MESH
PACK = 8
PIECE = 512


def ring_order(chips, rows):
    if rows == 2 and chips % 2 == 0:
        length = chips // 2
        return [z * 2 for z in range(length)] + [z * 2 + 1 for z in reversed(range(length))]
    return list(range(chips))


def lookup(index, table):
    found = jnp.int32(0)
    for at, value in enumerate(table):
        found = found + jnp.where(index == at, value, 0)
    return found


def column(row, rows):
    at = lax.broadcasted_iota(jnp.int32, (rows, rows), 0)
    to = lax.broadcasted_iota(jnp.int32, (rows, rows), 1)
    return jnp.sum(jnp.where(at == to, jnp.broadcast_to(row, (rows, rows)), jnp.zeros((), row.dtype)), axis=1, keepdims=True)


def kernel(order, tok_hbm, routes_hbm, gates_hbm, wg_hbm, wu_hbm, wd_hbm, out_ref,
           wg, wu, wd, routes_ref, gates_ref, x, tab, hid, mine, to_sib, from_sib, in_r, in_l, out_r, out_l,
           w_sem, t_sem, ag_send, ag_recv, sf_send, sf_recv, rs_send, rs_recv, ps_send, ps_recv, ready, turn):
    chips = len(order)
    half = chips // 2
    experts = 2 * chips
    rows, width = tok_hbm.shape
    ff = wg.shape[1]
    pieces = width // PIECE
    me = lax.axis_index("node")
    chip, core = me // 2, me % 2
    after, before = [0] * chips, [0] * chips
    for at in range(chips):
        after[order[at]] = order[(at + 1) % chips]
        before[order[at]] = order[(at - 1) % chips]
    right = lookup(chip, after) * 2 + core
    left = lookup(chip, before) * 2 + core
    sib = chip * 2 + (1 - core)

    barrier = pltpu.get_barrier_semaphore()
    for peer in (right, left):
        pl.semaphore_signal(barrier, inc=1, device_id={"node": peer}, device_id_type=MESH)

    @pl.when(core == 0)
    def _():
        pl.semaphore_signal(barrier, inc=1, device_id={"node": sib}, device_id_type=MESH)

    lanes = PACK * experts
    lane = lax.broadcasted_iota(jnp.int32, (rows, lanes), 1)
    sub = lax.broadcasted_iota(jnp.int32, (rows, lanes), 0) % PACK

    def place(offset):
        if offset == 0:
            return 0
        return 2 * offset - 1 if offset > 0 else -2 * offset

    def offset_of(way, d):
        return half if d == half else (-d if way == 0 else d)

    def remote(src, dst, send, recv, peer):
        return pltpu.make_async_remote_copy(src_ref=src, dst_ref=dst, send_sem=send, recv_sem=recv,
                                            device_id={"node": peer}, device_id_type=MESH)

    def program(own):
        other = 1 - own
        started = []

        def go(copy):
            copy.start()
            started.append(copy)

        local = [pltpu.make_async_copy(routes_hbm, routes_ref, t_sem.at[0]),
                 pltpu.make_async_copy(gates_hbm, gates_ref, t_sem.at[1]),
                 pltpu.make_async_copy(tok_hbm, x.at[own, pl.ds(0, rows), :], t_sem.at[2])]
        loads = [pltpu.make_async_copy(src, dst, w_sem.at[at])
                 for at, (src, dst) in enumerate(((wg_hbm, wg), (wu_hbm, wu), (wd_hbm, wd)))]

        def table():
            local[0].wait()
            local[1].wait()
            spread = jnp.zeros((rows, lanes), jnp.float32)
            for k in range(routes_ref.shape[0]):
                route, gate = column(routes_ref[k:k + 1, :], rows), column(gates_ref[k:k + 1, :], rows)
                spread = spread + jnp.where(lane == sub * experts + route, gate, 0.0)
            for at in range(rows // PACK):
                tab[own, 0, at:at + 1, :] = jnp.sum(spread[at * PACK:(at + 1) * PACK], axis=0, keepdims=True)

        def side(piece):
            return pl.ds(piece * PIECE, PIECE)

        def part(block, piece):
            return x.at[own, pl.ds(block * rows, rows), side(piece)]

        def hop(way, d, piece):
            to = place(offset_of(way, d))
            at = place(offset_of(way, d - 1)) if d > 1 else 0
            if piece == pieces:
                src, dst = tab.at[own, at], tab.at[own, to]
            else:
                src = tok_hbm.at[:, side(piece)] if d == 1 else part(at, piece)
                dst = part(to, piece)
            return remote(src, dst, ag_send.at[way, d - 1, piece], ag_recv.at[way, d - 1, piece], (right, left)[way])

        def travels(way, d, piece):
            if d < half:
                return True
            return way == (0 if piece == pieces else piece % 2)

        def arrive(d, piece):
            for way in (0, 1):
                if not travels(way, d, piece):
                    continue
                hop(way, d, piece).wait_recv()
                if d < half and travels(way, d + 1, piece):
                    go(hop(way, d + 1, piece))

        def group(d):
            if d == 2:
                return 0, 5
            return 2 * d - 1, (1 if d == half else 2)

        def share(wave, d):
            first, count = group(d)
            block = pl.ds(first * rows, count * rows)
            return [remote(x.at[wave, block, :], x.at[wave, block, :], sf_send.at[d - 2, 0], sf_recv.at[d - 2, 0], sib),
                    remote(tab.at[wave, pl.ds(first, count)], tab.at[wave, pl.ds(first, count)],
                           sf_send.at[d - 2, 1], sf_recv.at[d - 2, 1], sib)]

        def pass_on(d):
            for copy in share(own, d):
                go(copy)

        def shared(*distances):
            for d in distances:
                for copy in share(other, d):
                    copy.wait_recv()

        parts = (group(2), (5, chips - 5))

        def rows_in(half_of):
            first, count = parts[half_of]
            return pl.ds(first * rows, count * rows)

        def go_up(wave, half_of, tile, i):
            cols = pl.ds(i * tile, tile)
            values = x.at[wave, rows_in(half_of), :]
            gate = jnp.dot(values[...], wg[:, cols], preferred_element_type=jnp.float32)
            upper = jnp.dot(values[...], wu[:, cols], preferred_element_type=jnp.float32)
            hid[rows_in(half_of), cols] = (gate / (1.0 + jnp.exp(-gate)) * upper).astype(jnp.bfloat16)

        def weights(wave, half_of):
            found = []
            first, count = parts[half_of]
            for block in range(first, first + count):
                packed = tab[wave, block]
                full = jnp.concatenate([jnp.broadcast_to(packed[at:at + 1, :], (PACK, lanes)) for at in range(rows // PACK)], axis=0)
                found.append(jnp.sum(jnp.where(lane == sub * experts + me, full, 0.0), axis=1, keepdims=True))
            return jnp.concatenate(found, axis=0)

        def go_down(wave, half_of, gains, piece):
            made = jnp.dot(hid[rows_in(half_of), :], wd[:, side(piece)], preferred_element_type=jnp.float32)
            made = made.astype(jnp.bfloat16).astype(jnp.float32) * gains
            if wave == own:
                mine[rows_in(half_of), side(piece)] = made
            else:
                to_sib[rows_in(half_of), side(piece)] = made.astype(jnp.bfloat16)

        def pair(half_of, piece):
            return remote(to_sib.at[rows_in(half_of), side(piece)], from_sib.at[rows_in(half_of), side(piece)],
                          ps_send.at[half_of, piece], ps_recv.at[half_of, piece], sib)

        def chain(way, d, piece):
            src = (out_r, out_l)[way].at[d - 1, :, side(piece)]
            dst = (in_r, in_l)[way].at[d - 1, :, side(piece)]
            return remote(src, dst, rs_send.at[way, d - 1, piece], rs_recv.at[way, d - 1, piece], (right, left)[way])

        def both(at, piece):
            rows_of = pl.ds(at * rows, rows)
            return mine[rows_of, side(piece)] + from_sib[rows_of, side(piece)].astype(jnp.float32)

        def add_on(step, piece):
            for way in (piece % 2, 1 - piece % 2):
                first = half if piece % 2 == way else half - 1
                d = first + 1 - step
                if d < 1:
                    continue
                total = both(place(offset_of(1 - way, d)), piece)
                if step > 1:
                    chain(way, d + 1, piece).wait_recv()
                    total = total + (in_r, in_l)[way][d, :, side(piece)].astype(jnp.float32)
                (out_r, out_l)[way][d - 1, :, side(piece)] = total.astype(jnp.bfloat16)
                go(chain(way, d, piece))

        def finish(piece):
            total = both(0, piece)
            for way in (0, 1):
                chain(way, 1, piece).wait_recv()
                total = total + (in_r, in_l)[way][0, :, side(piece)].astype(jnp.float32)
            out_ref[:, side(piece)] = total.astype(jnp.bfloat16)

        def interleaved(events, of):
            done = [0]

            def run(upto):
                upto = len(events) if upto is None else len(events) * upto // of
                for event in events[done[0]:upto]:
                    event()
                done[0] = max(done[0], upto)
            return run

        def multiply(wave, half_of, tile_up, run=None, upto=(0,) * 11):
            run = run or (lambda count: None)
            ups = ff // tile_up
            for i in range(ups):
                go_up(wave, half_of, tile_up, i)
                run(upto[(i + 1) * 4 // ups - 1])
            loaded(2)
            gains = weights(wave, half_of)
            for piece in range(pieces):
                go_down(wave, half_of, gains, piece)
                if wave == other:
                    go(pair(half_of, piece))
                elif half_of == 1 and piece > 0:
                    joined(piece - 1)
                run(upto[4 + piece * 7 // pieces])
            if wave == own and half_of == 1:
                joined(pieces - 1)

        def joined(piece):
            for half_of in (0, 1):
                pair(half_of, piece).wait_recv()
            add_on(1, piece)

        for copy in local:
            copy.start()
        if own == 1:
            for load in loads:
                load.start()

        def first_hops():
            for piece in range(pieces):
                for way in (0, 1):
                    go(hop(way, 1, piece))

        def first_table_hops():
            for way in (0, 1):
                go(hop(way, 1, pieces))

        waited = set()

        def loaded(*which):
            for at in which:
                if at not in waited:
                    loads[at].wait()
                    waited.add(at)

        def arrivals(d):
            found = [functools.partial(arrive, d, piece) for piece in range(pieces)]

            def rest():
                arrive(d, pieces)
                if d >= 2:
                    pass_on(d)
            return found + [rest]

        def steps(step):
            return [functools.partial(add_on, step, piece) for piece in range(pieces)]

        if own == 0:
            pl.semaphore_wait(barrier, 2)
            first_hops()
            for load in loads:
                load.start()
            table()
            first_table_hops()
            local[2].wait()
            for event in arrivals(1):
                event()
            events = arrivals(2)
            for event in events[:-1]:
                event()
            pl.semaphore_wait(ready, 1)
            pl.semaphore_signal(turn, inc=1, device_id={"node": sib}, device_id_type=MESH)
            events[-1]()
            run = interleaved([e for d in range(3, half + 1) for e in arrivals(d)], 16)
            loaded(0, 1)
            multiply(0, 0, 256, run, (1, 3, 5, 7, 8, 8, 9, 10, 11, 12, 13))
            run(None)
            multiply(0, 1, 512)
            run = interleaved([e for step in range(2, half + 1) for e in steps(step)], 21)
            shared(2)
            multiply(1, 0, 256, run, (0, 1, 3, 5, 6, 7, 7, 8, 9, 10, 11))
            shared(*range(3, half + 1))
            multiply(1, 1, 512, run, (11, 12, 13, 14, 14, 15, 15, 16, 16, 17, 17))
            run(None)
        else:
            pl.semaphore_wait(barrier, 3)
            pl.semaphore_signal(ready, inc=1, device_id={"node": sib}, device_id_type=MESH)
            table()
            local[2].wait()
            pl.semaphore_wait(turn, 1)
            first_hops()
            first_table_hops()
            run = interleaved([e for d in range(1, half + 1) for e in arrivals(d)], 32)
            loaded(0, 1)
            shared(2)
            multiply(0, 0, 256, run, (0, 2, 4, 7, 8, 8, 9, 9, 10, 10, 11))
            shared(*range(3, half + 1))
            multiply(0, 1, 256, run, (14, 16, 18, 20, 20, 21, 21, 22, 22, 23, 23))
            multiply(1, 0, 256, run, (24, 27, 30, 32, 32, 32, 32, 32, 32, 32, 32))
            run(None)
            multiply(1, 1, 512)
            for step in range(2, half + 1):
                for event in steps(step):
                    event()
        for piece in range(pieces):
            finish(piece)
        for copy in started:
            copy.wait_send()

    for own in (0, 1):
        pl.when(core == own)(functools.partial(program, own))


def local(order, tokens, routes, gates, w_gate, w_up, w_down):
    rows, width = tokens.shape
    ff = w_gate.shape[2]
    chips = len(order)
    half = chips // 2
    pieces = width // PIECE
    bf16, f32 = jnp.bfloat16, jnp.float32
    dma = pltpu.SemaphoreType.DMA
    vmem = pl.BlockSpec(memory_space=pltpu.VMEM)
    hbm = pl.BlockSpec(memory_space=pl.ANY)
    return pl.pallas_call(
        functools.partial(kernel, order),
        out_shape=pltpu.VMEM((rows, width), bf16),
        in_specs=[hbm] * 6,
        out_specs=vmem,
        scratch_shapes=[
            pltpu.VMEM((width, ff), bf16),
            pltpu.VMEM((width, ff), bf16),
            pltpu.VMEM((ff, width), bf16),
            pltpu.VMEM(routes.shape[::-1], jnp.int32),
            pltpu.VMEM(gates.shape[::-1], f32),
            pltpu.VMEM((2, chips * rows, width), bf16),
            pltpu.VMEM((2, chips, rows // PACK, PACK * 2 * chips), f32),
            pltpu.VMEM((chips * rows, ff), bf16),
            pltpu.VMEM((chips * rows, width), f32),
            pltpu.VMEM((chips * rows, width), bf16),
            pltpu.VMEM((chips * rows, width), bf16),
            pltpu.VMEM((half, rows, width), bf16),
            pltpu.VMEM((half, rows, width), bf16),
            pltpu.VMEM((half, rows, width), bf16),
            pltpu.VMEM((half, rows, width), bf16),
            dma((3,)),
            dma((3,)),
            dma((2, half, pieces + 1)),
            dma((2, half, pieces + 1)),
            dma((half - 1, 2)),
            dma((half - 1, 2)),
            dma((2, half, pieces)),
            dma((2, half, pieces)),
            dma((2, pieces)),
            dma((2, pieces)),
            pltpu.SemaphoreType.REGULAR,
            pltpu.SemaphoreType.REGULAR,
        ],
        compiler_params=pltpu.CompilerParams(
            collective_id=0, has_side_effects=True, vmem_limit_bytes=58720256
        ),
    )(tokens, routes.T, gates.T, w_gate[0], w_up[0], w_down[0])


def solution(mesh):
    order = ring_order(mesh.shape["node"] // 2, 4 // mesh.shape["groups"])
    in_specs = (
        P(("groups", "node"), None),
        P(("groups", "node"), None),
        P(("groups", "node"), None),
        P("node", None, None),
        P("node", None, None),
        P("node", None, None),
    )
    out_specs = P(("groups", "node"), None)
    return jax.shard_map(
        functools.partial(local, order), mesh=mesh, in_specs=in_specs, out_specs=out_specs, check_vma=False
    )
```

```python
import functools

import jax
import jax.numpy as jnp
from jax import lax
from jax.experimental import pallas as pl
from jax.experimental.pallas import tpu as pltpu
from jax.sharding import PartitionSpec as P

MESH = pl.DeviceIdType.MESH
PACK = 8
PIECE = 512


def ring_order(chips, rows):
    if rows == 2 and chips % 2 == 0:
        length = chips // 2
        return [z * 2 for z in range(length)] + [z * 2 + 1 for z in reversed(range(length))]
    return list(range(chips))


def lookup(index, table):
    found = jnp.int32(0)
    for at, value in enumerate(table):
        found = found + jnp.where(index == at, value, 0)
    return found


def column(row, rows):
    at = lax.broadcasted_iota(jnp.int32, (rows, rows), 0)
    to = lax.broadcasted_iota(jnp.int32, (rows, rows), 1)
    return jnp.sum(jnp.where(at == to, jnp.broadcast_to(row, (rows, rows)), jnp.zeros((), row.dtype)), axis=1, keepdims=True)


def kernel(order, tok_hbm, routes_hbm, gates_hbm, wg_hbm, wu_hbm, wd_hbm, out_ref,
           wg, wu, wd, routes_ref, gates_ref, x, tab, hid, mine, to_sib, from_sib, in_r, in_l, out_r, out_l,
           w_sem, t_sem, ag_send, ag_recv, sf_send, sf_recv, rs_send, rs_recv, ps_send, ps_recv, ready, turn):
    chips = len(order)
    half = chips // 2
    experts = 2 * chips
    rows, width = tok_hbm.shape
    ff = wg.shape[1]
    pieces = width // PIECE
    me = lax.axis_index("node")
    chip, core = me // 2, me % 2
    after, before = [0] * chips, [0] * chips
    for at in range(chips):
        after[order[at]] = order[(at + 1) % chips]
        before[order[at]] = order[(at - 1) % chips]
    right = lookup(chip, after) * 2 + core
    left = lookup(chip, before) * 2 + core
    sib = chip * 2 + (1 - core)

    barrier = pltpu.get_barrier_semaphore()
    for peer in (right, left):
        pl.semaphore_signal(barrier, inc=1, device_id={"node": peer}, device_id_type=MESH)

    @pl.when(core == 0)
    def _():
        pl.semaphore_signal(barrier, inc=1, device_id={"node": sib}, device_id_type=MESH)

    lanes = PACK * experts
    lane = lax.broadcasted_iota(jnp.int32, (rows, lanes), 1)
    sub = lax.broadcasted_iota(jnp.int32, (rows, lanes), 0) % PACK

    def place(offset):
        if offset == 0:
            return 0
        return 2 * offset - 1 if offset > 0 else -2 * offset

    def offset_of(way, d):
        return half if d == half else (-d if way == 0 else d)

    def remote(src, dst, send, recv, peer):
        return pltpu.make_async_remote_copy(src_ref=src, dst_ref=dst, send_sem=send, recv_sem=recv,
                                            device_id={"node": peer}, device_id_type=MESH)

    def program(own):
        other = 1 - own
        started = []

        def go(copy):
            copy.start()
            started.append(copy)

        local = [pltpu.make_async_copy(routes_hbm, routes_ref, t_sem.at[0]),
                 pltpu.make_async_copy(gates_hbm, gates_ref, t_sem.at[1]),
                 pltpu.make_async_copy(tok_hbm, x.at[own, pl.ds(0, rows), :], t_sem.at[2])]
        loads = [pltpu.make_async_copy(src, dst, w_sem.at[at])
                 for at, (src, dst) in enumerate(((wg_hbm, wg), (wu_hbm, wu), (wd_hbm, wd)))]

        def table():
            local[0].wait()
            local[1].wait()
            spread = jnp.zeros((rows, lanes), jnp.float32)
            for k in range(routes_ref.shape[0]):
                route, gate = column(routes_ref[k:k + 1, :], rows), column(gates_ref[k:k + 1, :], rows)
                spread = spread + jnp.where(lane == sub * experts + route, gate, 0.0)
            for at in range(rows // PACK):
                tab[own, 0, at:at + 1, :] = jnp.sum(spread[at * PACK:(at + 1) * PACK], axis=0, keepdims=True)

        def side(piece):
            return pl.ds(piece * PIECE, PIECE)

        def part(block, piece):
            return x.at[own, pl.ds(block * rows, rows), side(piece)]

        def hop(way, d, piece):
            to = place(offset_of(way, d))
            at = place(offset_of(way, d - 1)) if d > 1 else 0
            if piece == pieces:
                src, dst = tab.at[own, at], tab.at[own, to]
            else:
                src = tok_hbm.at[:, side(piece)] if d == 1 else part(at, piece)
                dst = part(to, piece)
            return remote(src, dst, ag_send.at[way, d - 1, piece], ag_recv.at[way, d - 1, piece], (right, left)[way])

        def travels(way, d, piece):
            if d < half:
                return True
            return way == (0 if piece == pieces else piece % 2)

        def arrive(d, piece):
            for way in (0, 1):
                if not travels(way, d, piece):
                    continue
                hop(way, d, piece).wait_recv()
                if d < half and travels(way, d + 1, piece):
                    go(hop(way, d + 1, piece))

        def group(d):
            if d == 2:
                return 0, 5
            return 2 * d - 1, (1 if d == half else 2)

        def share(wave, d):
            first, count = group(d)
            block = pl.ds(first * rows, count * rows)
            return [remote(x.at[wave, block, :], x.at[wave, block, :], sf_send.at[d - 2, 0], sf_recv.at[d - 2, 0], sib),
                    remote(tab.at[wave, pl.ds(first, count)], tab.at[wave, pl.ds(first, count)],
                           sf_send.at[d - 2, 1], sf_recv.at[d - 2, 1], sib)]

        def pass_on(d):
            for copy in share(own, d):
                go(copy)

        def shared(*distances):
            for d in distances:
                for copy in share(other, d):
                    copy.wait_recv()

        parts = (group(2), (5, chips - 5))

        def rows_in(half_of):
            first, count = parts[half_of]
            return pl.ds(first * rows, count * rows)

        def go_up(wave, half_of, tile, i):
            cols = pl.ds(i * tile, tile)
            values = x.at[wave, rows_in(half_of), :]
            gate = jnp.dot(values[...], wg[:, cols], preferred_element_type=jnp.float32)
            upper = jnp.dot(values[...], wu[:, cols], preferred_element_type=jnp.float32)
            hid[rows_in(half_of), cols] = (gate / (1.0 + jnp.exp(-gate)) * upper).astype(jnp.bfloat16)

        def weights(wave, half_of):
            found = []
            first, count = parts[half_of]
            for block in range(first, first + count):
                packed = tab[wave, block]
                full = jnp.concatenate([jnp.broadcast_to(packed[at:at + 1, :], (PACK, lanes)) for at in range(rows // PACK)], axis=0)
                found.append(jnp.sum(jnp.where(lane == sub * experts + me, full, 0.0), axis=1, keepdims=True))
            return jnp.concatenate(found, axis=0)

        def go_down(wave, half_of, gains, piece):
            made = jnp.dot(hid[rows_in(half_of), :], wd[:, side(piece)], preferred_element_type=jnp.float32)
            made = made.astype(jnp.bfloat16).astype(jnp.float32) * gains
            if wave == own:
                mine[rows_in(half_of), side(piece)] = made
            else:
                to_sib[rows_in(half_of), side(piece)] = made.astype(jnp.bfloat16)

        def pair(half_of, piece):
            return remote(to_sib.at[rows_in(half_of), side(piece)], from_sib.at[rows_in(half_of), side(piece)],
                          ps_send.at[half_of, piece], ps_recv.at[half_of, piece], sib)

        def chain(way, d, piece):
            src = (out_r, out_l)[way].at[d - 1, :, side(piece)]
            dst = (in_r, in_l)[way].at[d - 1, :, side(piece)]
            return remote(src, dst, rs_send.at[way, d - 1, piece], rs_recv.at[way, d - 1, piece], (right, left)[way])

        def both(at, piece):
            rows_of = pl.ds(at * rows, rows)
            return mine[rows_of, side(piece)] + from_sib[rows_of, side(piece)].astype(jnp.float32)

        def add_on(step, piece):
            for way in (piece % 2, 1 - piece % 2):
                first = half if piece % 2 == way else half - 1
                d = first + 1 - step
                if d < 1:
                    continue
                total = both(place(offset_of(1 - way, d)), piece)
                if step > 1:
                    chain(way, d + 1, piece).wait_recv()
                    total = total + (in_r, in_l)[way][d, :, side(piece)].astype(jnp.float32)
                (out_r, out_l)[way][d - 1, :, side(piece)] = total.astype(jnp.bfloat16)
                go(chain(way, d, piece))

        def finish(piece):
            total = both(0, piece)
            for way in (0, 1):
                chain(way, 1, piece).wait_recv()
                total = total + (in_r, in_l)[way][0, :, side(piece)].astype(jnp.float32)
            out_ref[:, side(piece)] = total.astype(jnp.bfloat16)

        def interleaved(events, of):
            done = [0]

            def run(upto):
                upto = len(events) if upto is None else len(events) * upto // of
                for event in events[done[0]:upto]:
                    event()
                done[0] = max(done[0], upto)
            return run

        def multiply(wave, half_of, tile_up, run=None, upto=(0,) * 11):
            run = run or (lambda count: None)
            ups = ff // tile_up
            for i in range(ups):
                go_up(wave, half_of, tile_up, i)
                run(upto[(i + 1) * 4 // ups - 1])
            loaded(2)
            gains = weights(wave, half_of)
            for piece in range(pieces):
                go_down(wave, half_of, gains, piece)
                if wave == other:
                    go(pair(half_of, piece))
                elif half_of == 1 and piece > 0:
                    joined(piece - 1)
                run(upto[4 + piece * 7 // pieces])
            if wave == own and half_of == 1:
                joined(pieces - 1)

        def joined(piece):
            for half_of in (0, 1):
                pair(half_of, piece).wait_recv()
            add_on(1, piece)

        for copy in local:
            copy.start()
        if own == 1:
            for load in loads:
                load.start()

        def first_hops():
            for piece in range(pieces):
                for way in (0, 1):
                    go(hop(way, 1, piece))

        def first_table_hops():
            for way in (0, 1):
                go(hop(way, 1, pieces))

        waited = set()

        def loaded(*which):
            for at in which:
                if at not in waited:
                    loads[at].wait()
                    waited.add(at)

        def arrivals(d):
            found = [functools.partial(arrive, d, piece) for piece in range(pieces)]

            def rest():
                arrive(d, pieces)
                if d >= 2:
                    pass_on(d)
            return found + [rest]

        def steps(step):
            return [functools.partial(add_on, step, piece) for piece in range(pieces)]

        if own == 0:
            pl.semaphore_wait(barrier, 2)
            first_hops()
            for load in loads:
                load.start()
            table()
            first_table_hops()
            local[2].wait()
            for event in arrivals(1):
                event()
            events = arrivals(2)
            for event in events[:-1]:
                event()
            pl.semaphore_wait(ready, 1)
            pl.semaphore_signal(turn, inc=1, device_id={"node": sib}, device_id_type=MESH)
            events[-1]()
            run = interleaved([e for d in range(3, half + 1) for e in arrivals(d)], 16)
            loaded(0, 1)
            multiply(0, 0, 256, run, (2, 5, 7, 8, 9, 10, 11, 12, 13, 14, 15))
            run(None)
            multiply(0, 1, 512)
            run = interleaved([e for step in range(2, half + 1) for e in steps(step)], 21)
            shared(2)
            multiply(1, 0, 256, run, (0, 1, 3, 5, 6, 7, 7, 8, 9, 10, 11))
            shared(*range(3, half + 1))
            multiply(1, 1, 512, run, (11, 12, 13, 14, 14, 15, 15, 16, 16, 17, 17))
            run(None)
        else:
            pl.semaphore_wait(barrier, 3)
            pl.semaphore_signal(ready, inc=1, device_id={"node": sib}, device_id_type=MESH)
            table()
            local[2].wait()
            pl.semaphore_wait(turn, 1)
            first_hops()
            first_table_hops()
            run = interleaved([e for d in range(1, half + 1) for e in arrivals(d)], 32)
            loaded(0, 1)
            shared(2)
            multiply(0, 0, 256, run, (0, 2, 4, 7, 8, 8, 9, 9, 10, 10, 11))
            shared(*range(3, half + 1))
            multiply(0, 1, 256, run, (14, 16, 18, 20, 20, 21, 21, 22, 22, 23, 23))
            multiply(1, 0, 256, run, (24, 27, 30, 32, 32, 32, 32, 32, 32, 32, 32))
            run(None)
            multiply(1, 1, 512)
            for step in range(2, half + 1):
                for event in steps(step):
                    event()
        for piece in range(pieces):
            finish(piece)
        for copy in started:
            copy.wait_send()

    for own in (0, 1):
        pl.when(core == own)(functools.partial(program, own))


def local(order, tokens, routes, gates, w_gate, w_up, w_down):
    rows, width = tokens.shape
    ff = w_gate.shape[2]
    chips = len(order)
    half = chips // 2
    pieces = width // PIECE
    bf16, f32 = jnp.bfloat16, jnp.float32
    dma = pltpu.SemaphoreType.DMA
    vmem = pl.BlockSpec(memory_space=pltpu.VMEM)
    hbm = pl.BlockSpec(memory_space=pl.ANY)
    return pl.pallas_call(
        functools.partial(kernel, order),
        out_shape=pltpu.VMEM((rows, width), bf16),
        in_specs=[hbm] * 6,
        out_specs=vmem,
        scratch_shapes=[
            pltpu.VMEM((width, ff), bf16),
            pltpu.VMEM((width, ff), bf16),
            pltpu.VMEM((ff, width), bf16),
            pltpu.VMEM(routes.shape[::-1], jnp.int32),
            pltpu.VMEM(gates.shape[::-1], f32),
            pltpu.VMEM((2, chips * rows, width), bf16),
            pltpu.VMEM((2, chips, rows // PACK, PACK * 2 * chips), f32),
            pltpu.VMEM((chips * rows, ff), bf16),
            pltpu.VMEM((chips * rows, width), f32),
            pltpu.VMEM((chips * rows, width), bf16),
            pltpu.VMEM((chips * rows, width), bf16),
            pltpu.VMEM((half, rows, width), bf16),
            pltpu.VMEM((half, rows, width), bf16),
            pltpu.VMEM((half, rows, width), bf16),
            pltpu.VMEM((half, rows, width), bf16),
            dma((3,)),
            dma((3,)),
            dma((2, half, pieces + 1)),
            dma((2, half, pieces + 1)),
            dma((half - 1, 2)),
            dma((half - 1, 2)),
            dma((2, half, pieces)),
            dma((2, half, pieces)),
            dma((2, pieces)),
            dma((2, pieces)),
            pltpu.SemaphoreType.REGULAR,
            pltpu.SemaphoreType.REGULAR,
        ],
        compiler_params=pltpu.CompilerParams(
            collective_id=0, has_side_effects=True, vmem_limit_bytes=58720256
        ),
    )(tokens, routes.T, gates.T, w_gate[0], w_up[0], w_down[0])


def solution(mesh):
    order = ring_order(mesh.shape["node"] // 2, 4 // mesh.shape["groups"])
    in_specs = (
        P(("groups", "node"), None),
        P(("groups", "node"), None),
        P(("groups", "node"), None),
        P("node", None, None),
        P("node", None, None),
        P("node", None, None),
    )
    out_specs = P(("groups", "node"), None)
    return jax.shard_map(
        functools.partial(local, order), mesh=mesh, in_specs=in_specs, out_specs=out_specs, check_vma=False
    )
```
